32 devices in a mesh: dp: 16 (over z, y, core), fsdp: 2 (over x).
Axes of the slice: x: 2, y: 2, z: 4, core: 2. Of those that a mesh axis runs over, the one named last changes fastest.
Arguments:
- hidden_in: bfloat16 [4096, 1024], P(('dp', 'fsdp')), may hold values from -6 to 6
- doc_id: int32 [4096], P(('dp', 'fsdp')), may hold values from 0 to 128, as said below
- expert_ids: int32 [4096, 8], P(('dp', 'fsdp')), may hold values from 0 to 15, all different within a row
- out_grad: bfloat16 [4096, 1024], P(('dp', 'fsdp')), may hold values from -6 to 6
- attn_gain: bfloat16 [1024], P(('dp', 'fsdp')), may hold values from 0.5 to 1.5
- query_weight: bfloat16 [1024, 1024], P(('dp', 'fsdp')), may hold values from -0.1875 to 0.1875
- key_weight: bfloat16 [1024, 512], P(('dp', 'fsdp')), may hold values from -0.1875 to 0.1875
- value_weight: bfloat16 [1024, 512], P(('dp', 'fsdp')), may hold values from -0.1875 to 0.1875
- output_weight: bfloat16 [1024, 1024], P(('dp', 'fsdp')), may hold values from -0.75 to 0.75
- ffn_gain: bfloat16 [1024], P(('dp', 'fsdp')), may hold values from 0.5 to 1.5
- router_weight: bfloat16 [1024, 16], P(('dp', 'fsdp')), may hold values from -0.375 to 0.375
- expert_gate: bfloat16 [16, 1024, 512], P('dp', 'fsdp'), may hold values from -0.1875 to 0.1875
- expert_up: bfloat16 [16, 1024, 512], P('dp', 'fsdp'), may hold values from -0.1875 to 0.1875
- expert_down: bfloat16 [16, 512, 1024], P('dp', 'fsdp'), may hold values from -1 to 1
Outputs:
- layer_out: bfloat16 [4096, 1024], P(('dp', 'fsdp'))
- grad_in: bfloat16 [4096, 1024], P(('dp', 'fsdp'))
- grad_attn_gain: float32 [1024], P(('dp', 'fsdp'))
- grad_query: float32 [1024, 1024], P(('dp', 'fsdp'))
- grad_key: float32 [1024, 512], P(('dp', 'fsdp'))
- grad_value: float32 [1024, 512], P(('dp', 'fsdp'))
- grad_output: float32 [1024, 1024], P(('dp', 'fsdp'))
- grad_ffn_gain: float32 [1024], P(('dp', 'fsdp'))
- grad_router: float32 [1024, 16], P(('dp', 'fsdp'))
- grad_expert_gate: float32 [16, 1024, 512], P('dp', 'fsdp')
- grad_expert_up: float32 [16, 1024, 512], P('dp', 'fsdp')
- grad_expert_down: float32 [16, 512, 1024], P('dp', 'fsdp')
The draws below stay inside these ranges and needn't reach their ends.
Inputs may be any that keep to these rules, and one draw needn't show every extreme that they name: Within each block of 128 rows doc_id starts at 0 and never falls; live rows come first and carry ids below 128; the rows after them carry 128 (padding). Every block has 64 or more live rows and some block has no padding. `expert_ids`: each row names 8 different experts.
All inputs are finite; a program needn't handle non-finite values.
Results may differ from the reference program's by a relative error of at most 0.015.
The reference program's roundings to bfloat16 on the way count: a program that leaves them out, or rounds other values in their place, can miss the bound.
Values may be sent and summed in bfloat16 or wider, within the bound.
A program may use at most 128 MiB of HBM per device.

```python
import jax
import jax.numpy as jnp
from jax import lax

D = 1024
HEADS = 16
KV_HEADS = 8
HEAD_DIM = 64
FF = 512
TOP = 8
TOK_DEV = 128
EXPERTS = 16
CAP = 24
TOKENS = 4096


def draw_doc_id(key, part):
    blocks = TOKENS // TOK_DEV
    key_live, key_full, key_cuts = jax.random.split(jax.random.fold_in(key, 17), 3)
    live_count = jax.random.randint(key_live, (blocks,), TOK_DEV // 2, TOK_DEV + 1)
    fullest = jax.random.randint(key_full, (), 0, blocks)
    live_count = jnp.where(jnp.arange(blocks) == fullest, TOK_DEV, live_count)
    cuts = jax.random.randint(key_cuts, (blocks, TOK_DEV), 0, 32)
    position = jnp.arange(TOK_DEV)
    starts = jnp.where(position[None, :] == 0, 1, (cuts == 0).astype(jnp.int32))
    numbers = jnp.cumsum(starts, axis=1) - 1
    numbers = jnp.where(position[None, :] < live_count[:, None], numbers, TOK_DEV)
    return numbers.reshape(TOKENS).astype(jnp.int32)


def shard_levels(key, shape, pieces, low, high):
    def one(dim, blocks):
        steps = jax.random.uniform(jax.random.fold_in(jax.random.fold_in(key, 6), dim), (blocks,), jnp.float32, low / len(pieces), high / len(pieces))
        return jnp.repeat(jnp.exp(steps), shape[dim] // blocks).reshape((-1,) + (1,) * (len(shape) - dim - 1))

    loudness = one(*pieces[0])
    for cut in pieces[1:]:
        loudness = loudness * one(*cut)
    return loudness


def choose_distinct(rng, rows, amount, top, lift):
    sequence = jax.random.permutation(jax.random.fold_in(rng, 1), amount)
    boost = sequence
    for power in range(3):
        boost = boost * boost // amount
    boost = boost * lift // amount
    tickets = jax.random.randint(jax.random.fold_in(rng, 2), (rows, amount), 0, 4096) + boost
    fixed_rows = jax.random.permutation(jax.random.fold_in(rng, 3), rows)[jnp.arange(amount) % rows]
    tickets = jnp.where(jnp.arange(rows)[:, None] == fixed_rows[None, :], 1 << 14, tickets)
    priority = tickets * amount + jnp.arange(amount)
    return lax.top_k(priority.astype(jnp.int32), top)[1].astype(jnp.int32)


def scatter_about(key, dims, scale, most, pieces=(), held_as=jnp.bfloat16):
    factor_of = shard_levels(key, dims, pieces, -0.22, 0.18) if pieces else 1.0
    drawn = jax.random.normal(key, dims, jnp.float32) * scale * factor_of
    return jnp.minimum(jnp.maximum(drawn, -most), most).astype(held_as)


def setup_inputs(seed: int = 0) -> dict:
    keys = jax.random.split(jax.random.key(seed), 15)
    hidden_in = scatter_about(keys[0], (TOKENS, D), 1.0, 6.0, ((0, 32),))
    doc_id = draw_doc_id(jax.random.fold_in(keys[14], 71), 0)
    expert_ids = choose_distinct(keys[2], TOKENS, EXPERTS, TOP, 4096)
    out_grad = scatter_about(keys[3], (TOKENS, D), 1.0, 6.0, ((0, 32),))
    attn_gain = jnp.clip(1.0 + 0.1 * jax.random.normal(keys[4], (D,), jnp.float32), 0.5, 1.5).astype(jnp.bfloat16)
    query_weight = scatter_about(keys[5], (D, HEADS * HEAD_DIM), D ** -0.5, 0.1875, ((0, 32),))
    key_weight = scatter_about(keys[6], (D, KV_HEADS * HEAD_DIM), D ** -0.5, 0.1875, ((0, 32),))
    value_weight = scatter_about(keys[7], (D, KV_HEADS * HEAD_DIM), D ** -0.5, 0.1875, ((0, 32),))
    output_weight = scatter_about(keys[8], (HEADS * HEAD_DIM, D), (D // 16) ** -0.5, 0.75, ((0, 32),))
    ffn_gain = jnp.clip(1.0 + 0.1 * jax.random.normal(keys[9], (D,), jnp.float32), 0.5, 1.5).astype(jnp.bfloat16)
    router_weight = scatter_about(keys[10], (D, EXPERTS), (D // 4) ** -0.5, 0.375, ((0, 32),))
    expert_gate = scatter_about(keys[11], (EXPERTS, D, FF), D ** -0.5, 0.1875, ((0, 16), (1, 2)))
    expert_up = scatter_about(keys[12], (EXPERTS, D, FF), D ** -0.5, 0.1875, ((0, 16), (1, 2)))
    expert_down = scatter_about(keys[13], (EXPERTS, FF, D), (FF // 16) ** -0.5, 1.0, ((0, 16), (1, 2)))
    return {"hidden_in": hidden_in, "doc_id": doc_id, "expert_ids": expert_ids, "out_grad": out_grad, "attn_gain": attn_gain, "query_weight": query_weight, "key_weight": key_weight, "value_weight": value_weight, "output_weight": output_weight, "ffn_gain": ffn_gain, "router_weight": router_weight, "expert_gate": expert_gate, "expert_up": expert_up, "expert_down": expert_down}


norm_eps = 1e-05

def round_half(values):
    return lax.optimization_barrier(values.astype(jnp.bfloat16))

def widen(values):
    return values.astype(jnp.float32)

def positions_mask(doc_block):
    row_count = doc_block.shape[0]
    row_index = jnp.arange(row_count)
    same_doc = doc_block[:, None] == doc_block[None, :]
    earlier = row_index[None, :] < row_index[:, None]
    position = lax.optimization_barrier(jnp.sum((same_doc & earlier).astype(jnp.float32), axis=1))
    allowed = same_doc & (row_index[None, :] <= row_index[:, None])
    live_rows = (doc_block < row_count).astype(jnp.float32)
    return (position, allowed, live_rows)

def rope_tables(position):
    half_dim = HEAD_DIM // 2
    freqs = jnp.exp(-jnp.log(10000.0) * (2.0 * jnp.arange(half_dim, dtype=jnp.float32) / HEAD_DIM))
    angle = position[:, None] * freqs[None, :]
    return (jnp.cos(angle), jnp.sin(angle))

def rotate(values, cosine, sinusoid):
    half_dim = values.shape[-1] // 2
    first_half, second_half = (values[..., :half_dim], values[..., half_dim:])
    return jnp.concatenate([first_half * cosine - second_half * sinusoid, second_half * cosine + first_half * sinusoid], axis=-1)

def unrotate(values, cosine, sinusoid):
    half_dim = values.shape[-1] // 2
    first_half, second_half = (values[..., :half_dim], values[..., half_dim:])
    return jnp.concatenate([first_half * cosine + second_half * sinusoid, second_half * cosine - first_half * sinusoid], axis=-1)

def norm_forward(values, gain):
    scale_row = lax.rsqrt(lax.optimization_barrier(jnp.mean(values * values, axis=-1, keepdims=True)) + norm_eps)
    normed = values * scale_row
    return (normed, scale_row, round_half(normed * gain))

def norm_backward(upstream, normed, scale_row, gain):
    scaled = upstream * gain
    inner = lax.optimization_barrier(jnp.mean(scaled * normed, axis=-1, keepdims=True))
    return (scale_row * (scaled - normed * inner), lax.optimization_barrier(jnp.sum(upstream * normed, axis=0)))

def probabilities(query_b, key_b, allowed, log_total):
    scores = jnp.einsum('ikgd,jkd->kgij', widen(query_b), widen(key_b)) * HEAD_DIM ** (-0.5)
    raised = jnp.where(allowed[None, None], jnp.exp(scores), 0.0)
    if log_total is None:
        log_total = jnp.log(lax.optimization_barrier(jnp.sum(raised, axis=-1, keepdims=True)))
    return (jnp.where(allowed[None, None], jnp.exp(scores - log_total), 0.0), log_total)

def routing(expert_block, live_rows, logits):
    experts = logits.shape[1]
    row_count = expert_block.shape[0]
    chosen = lax.optimization_barrier(jnp.sum((expert_block[:, :, None] == jnp.arange(experts)[None, None, :]).astype(jnp.float32), axis=1))
    raised = jnp.where(chosen > 0, jnp.exp(logits), 0.0)
    gates = raised / lax.optimization_barrier(jnp.sum(raised, axis=1, keepdims=True))
    member = chosen * live_rows[:, None]
    lower = (jnp.arange(row_count)[None, :] < jnp.arange(row_count)[:, None]).astype(jnp.float32)
    rank = jnp.dot(lower, member, precision=lax.Precision.HIGHEST)
    kept = member * (rank < CAP).astype(jnp.float32)
    slot_match = (rank.T[:, None, :] == jnp.arange(CAP, dtype=jnp.float32)[None, :, None]).astype(jnp.float32)
    dispatch = kept.T[:, None, :] * slot_match
    return (gates, dispatch)

def reference(hidden_in, doc_id, expert_ids, out_grad, attn_gain, query_weight, key_weight, value_weight, output_weight, ffn_gain, router_weight, expert_gate, expert_up, expert_down):
    blocks = TOKENS // TOK_DEV
    groups = HEADS // KV_HEADS
    scale = HEAD_DIM ** (-0.5)
    gate_wide = widen(expert_gate)
    up_wide = widen(expert_up)
    down_wide = widen(expert_down)
    gain_one = widen(attn_gain)
    gain_two = widen(ffn_gain)

    def one_block(totals, inputs):
        hidden_blk, doc_blk, ids_blk, grad_blk = inputs
        rows = hidden_blk.shape[0]
        position, allowed, live_rows = positions_mask(doc_blk)
        cosine, sinusoid = rope_tables(position)
        cos_query, sin_query = (cosine[:, None, None, :], sinusoid[:, None, None, :])
        cos_key, sin_key = (cosine[:, None, :], sinusoid[:, None, :])
        resid_in = widen(hidden_blk)
        normed_one, scale_one, normed_in = norm_forward(resid_in, gain_one)
        query_raw = jnp.dot(normed_in, query_weight, preferred_element_type=jnp.float32).reshape(rows, KV_HEADS, groups, HEAD_DIM)
        key_raw = jnp.dot(normed_in, key_weight, preferred_element_type=jnp.float32).reshape(rows, KV_HEADS, HEAD_DIM)
        query_b = round_half(rotate(query_raw, cos_query, sin_query))
        key_b = round_half(rotate(key_raw, cos_key, sin_key))
        value_b = round_half(jnp.dot(normed_in, value_weight, preferred_element_type=jnp.float32).reshape(rows, KV_HEADS, HEAD_DIM))
        probs, log_total = probabilities(query_b, key_b, allowed, None)
        probs_b = round_half(probs)
        mixed = jnp.einsum('kgij,jkd->ikgd', widen(probs_b), widen(value_b))
        mixed_b = round_half((mixed * live_rows[:, None, None, None]).reshape(rows, D))
        resid_mid = resid_in + jnp.dot(mixed_b, output_weight, preferred_element_type=jnp.float32)
        normed_two, scale_two, routed_in = norm_forward(resid_mid, gain_two)
        logits = jnp.dot(routed_in, router_weight, preferred_element_type=jnp.float32)
        gates, dispatch = routing(ids_blk, live_rows, logits)
        send_rows = round_half(jnp.einsum('ecr,rd->ecd', dispatch, widen(routed_in)))
        gate_pre = jnp.einsum('ecd,edf->ecf', widen(send_rows), gate_wide)
        up_pre = jnp.einsum('ecd,edf->ecf', widen(send_rows), up_wide)
        act_rows = round_half(jax.nn.silu(gate_pre) * up_pre)
        out_rows = round_half(jnp.einsum('ecf,efd->ecd', widen(act_rows), down_wide))
        combine = dispatch * gates.T[:, None, :]
        expert_sum = jnp.einsum('ecr,ecd->rd', combine, widen(out_rows), precision=lax.Precision.HIGHEST)
        layer_out = (resid_mid + expert_sum).astype(jnp.bfloat16)
        grad_out = widen(grad_blk)
        grad_send = round_half(jnp.einsum('ecr,rd->ecd', combine, grad_out, precision=lax.Precision.HIGHEST))
        row_dots = jnp.einsum('ecd,rd->ecr', widen(out_rows), grad_out, precision=lax.Precision.HIGHEST)
        grad_gates = lax.optimization_barrier(jnp.sum(dispatch * row_dots, axis=1)).T
        grad_logits = gates * (grad_gates - lax.optimization_barrier(jnp.sum(gates * grad_gates, axis=1, keepdims=True)))
        grad_logits_b = round_half(grad_logits)
        grad_act = jnp.einsum('ecd,efd->ecf', widen(grad_send), down_wide)
        sigmoid_gate = jax.nn.sigmoid(gate_pre)
        grad_up_pre = round_half(grad_act * gate_pre * sigmoid_gate)
        grad_gate_pre = round_half(grad_act * up_pre * sigmoid_gate * (1.0 + gate_pre * (1.0 - sigmoid_gate)))
        grad_down_w = jnp.einsum('ecf,ecd->efd', widen(act_rows), widen(grad_send))
        grad_gate_w = jnp.einsum('ecd,ecf->edf', widen(send_rows), widen(grad_gate_pre))
        grad_up_w = jnp.einsum('ecd,ecf->edf', widen(send_rows), widen(grad_up_pre))
        grad_rows_in = round_half(jnp.einsum('ecf,edf->ecd', widen(grad_gate_pre), gate_wide) + jnp.einsum('ecf,edf->ecd', widen(grad_up_pre), up_wide))
        grad_routed = jnp.einsum('ecr,ecd->rd', dispatch, widen(grad_rows_in)) + jnp.dot(grad_logits_b, router_weight.T, preferred_element_type=jnp.float32)
        grad_w_router = jnp.dot(routed_in.T, grad_logits_b, preferred_element_type=jnp.float32)
        grad_norm_two, grad_gain_two = norm_backward(grad_routed, normed_two, scale_two, gain_two)
        grad_mid = grad_out + grad_norm_two
        grad_mid_b = round_half(grad_mid)
        grad_w_output = jnp.dot(mixed_b.T, grad_mid_b, preferred_element_type=jnp.float32)
        grad_mixed = round_half(jnp.dot(grad_mid_b, output_weight.T, preferred_element_type=jnp.float32).reshape(rows, KV_HEADS, groups, HEAD_DIM) * live_rows[:, None, None, None])
        probs_again, unused_total = probabilities(query_b, key_b, allowed, log_total)
        grad_probs = jnp.einsum('ikgd,jkd->kgij', widen(grad_mixed), widen(value_b))
        delta = lax.optimization_barrier(jnp.sum(probs_again * grad_probs, axis=-1, keepdims=True))
        grad_scores = round_half(probs_again * (grad_probs - delta) * scale)
        grad_query_raw = jnp.einsum('kgij,jkd->ikgd', widen(grad_scores), widen(key_b))
        grad_key_raw = jnp.einsum('kgij,ikgd->jkd', widen(grad_scores), widen(query_b))
        grad_value_raw = jnp.einsum('kgij,ikgd->jkd', widen(probs_b), widen(grad_mixed))
        grad_query_b = round_half(unrotate(grad_query_raw, cos_query, sin_query).reshape(rows, HEADS * HEAD_DIM))
        grad_key_b = round_half(unrotate(grad_key_raw, cos_key, sin_key).reshape(rows, KV_HEADS * HEAD_DIM))
        grad_value_b = round_half(grad_value_raw.reshape(rows, KV_HEADS * HEAD_DIM))
        grad_w_query = jnp.dot(normed_in.T, grad_query_b, preferred_element_type=jnp.float32)
        grad_w_key = jnp.dot(normed_in.T, grad_key_b, preferred_element_type=jnp.float32)
        grad_w_value = jnp.dot(normed_in.T, grad_value_b, preferred_element_type=jnp.float32)
        grad_normed = jnp.dot(grad_query_b, query_weight.T, preferred_element_type=jnp.float32)
        grad_normed = grad_normed + jnp.dot(grad_key_b, key_weight.T, preferred_element_type=jnp.float32)
        grad_normed = grad_normed + jnp.dot(grad_value_b, value_weight.T, preferred_element_type=jnp.float32)
        grad_norm_one, grad_gain_one = norm_backward(grad_normed, normed_one, scale_one, gain_one)
        grad_input = (grad_mid + grad_norm_one).astype(jnp.bfloat16)
        terms = (grad_gain_one, grad_w_query, grad_w_key, grad_w_value, grad_w_output, grad_gain_two, grad_w_router, grad_gate_w, grad_up_w, grad_down_w)
        new_totals = tuple((total + term for total, term in zip(totals, terms)))
        return (new_totals, (layer_out, grad_input))
    experts = router_weight.shape[1]
    zeros_init = (jnp.zeros((D,), jnp.float32), jnp.zeros((D, HEADS * HEAD_DIM), jnp.float32), jnp.zeros((D, KV_HEADS * HEAD_DIM), jnp.float32), jnp.zeros((D, KV_HEADS * HEAD_DIM), jnp.float32), jnp.zeros((HEADS * HEAD_DIM, D), jnp.float32), jnp.zeros((D,), jnp.float32), jnp.zeros((D, experts), jnp.float32), jnp.zeros((experts, D, FF), jnp.float32), jnp.zeros((experts, D, FF), jnp.float32), jnp.zeros((experts, FF, D), jnp.float32))
    inputs = (hidden_in.reshape(blocks, TOK_DEV, D), doc_id.reshape(blocks, TOK_DEV), expert_ids.reshape(blocks, TOK_DEV, TOP), out_grad.reshape(blocks, TOK_DEV, D))
    totals, (layer_out, grad_input) = lax.scan(one_block, zeros_init, inputs)
    return (layer_out.reshape(TOKENS, D), grad_input.reshape(TOKENS, D), totals[0], totals[1], totals[2], totals[3], totals[4], totals[5], totals[6], totals[7], totals[8], totals[9])
```

```python
import functools

import jax
import jax.numpy as jnp
from jax import lax
from jax.experimental import pallas as pl
from jax.experimental.pallas import tpu as pltpu
from jax.sharding import PartitionSpec as P

HEADS = 16
KV_HEADS = 8
HEAD_DIM = 64
TOP = 8
CAP = 24


norm_eps = 1e-05


def positions_mask(doc_block):
    row_count = doc_block.shape[0]
    row_index = jnp.arange(row_count)
    same_doc = doc_block[:, None] == doc_block[None, :]
    earlier = row_index[None, :] < row_index[:, None]
    position = jnp.sum((same_doc & earlier).astype(jnp.float32), axis=1)
    allowed = same_doc & (row_index[None, :] <= row_index[:, None])
    live_rows = (doc_block < row_count).astype(jnp.float32)
    return (position, allowed, live_rows)


def rope_tables(position):
    half_dim = HEAD_DIM // 2
    freqs = jnp.exp(-jnp.log(10000.0) * (2.0 * jnp.arange(half_dim, dtype=jnp.float32) / HEAD_DIM))
    angle = position[:, None] * freqs[None, :]
    return (jnp.cos(angle), jnp.sin(angle))


def rotate(values, cosine, sinusoid):
    half_dim = values.shape[-1] // 2
    first_half, second_half = (values[..., :half_dim], values[..., half_dim:])
    return jnp.concatenate(
        [
            first_half * cosine - second_half * sinusoid,
            second_half * cosine + first_half * sinusoid,
        ],
        axis=-1,
    )


def unrotate(values, cosine, sinusoid):
    half_dim = values.shape[-1] // 2
    first_half, second_half = (values[..., :half_dim], values[..., half_dim:])
    return jnp.concatenate(
        [
            first_half * cosine + second_half * sinusoid,
            second_half * cosine - first_half * sinusoid,
        ],
        axis=-1,
    )


def norm_forward(values, gain):
    scale_row = lax.rsqrt(jnp.mean(values * values, axis=-1, keepdims=True) + norm_eps)
    normed = values * scale_row
    return (normed, scale_row, (normed * gain).astype(jnp.bfloat16))


def norm_backward(upstream, normed, scale_row, gain):
    scaled = upstream * gain
    inner = jnp.mean(scaled * normed, axis=-1, keepdims=True)
    return (scale_row * (scaled - normed * inner), jnp.sum(upstream * normed, axis=0))


def probabilities(query_b, key_b, allowed, log_total):
    scores = jnp.einsum(
        "ikgd,jkd->kgij", query_b, key_b, preferred_element_type=jnp.float32
    ) * HEAD_DIM ** (-0.5)
    raised = jnp.where(allowed[None, None], jnp.exp(scores), 0.0)
    if log_total is None:
        log_total = jnp.log(jnp.sum(raised, axis=-1, keepdims=True))
    return (jnp.where(allowed[None, None], jnp.exp(scores - log_total), 0.0), log_total)


def routing(expert_block, live_rows, logits):
    experts = logits.shape[1]
    row_count = expert_block.shape[0]
    chosen = jnp.sum(
        (expert_block[:, :, None] == jnp.arange(experts)[None, None, :]).astype(jnp.float32), axis=1
    )
    raised = jnp.where(chosen > 0, jnp.exp(logits), 0.0)
    gates = raised / jnp.sum(raised, axis=1, keepdims=True)
    member = chosen * live_rows[:, None]
    lower = (jnp.arange(row_count)[None, :] < jnp.arange(row_count)[:, None]).astype(jnp.float32)
    rank = jnp.dot(lower, member, precision=lax.Precision.HIGHEST)
    kept = member * (rank < CAP).astype(jnp.float32)
    slot_match = (rank.T[:, None, :] == jnp.arange(CAP, dtype=jnp.float32)[None, :, None]).astype(
        jnp.float32
    )
    dispatch = kept.T[:, None, :] * slot_match
    return (gates, dispatch, kept, rank)


def expert_forward(rows_in, w_gate, w_up, w_down):
    gate_pre = jnp.dot(rows_in, w_gate, preferred_element_type=jnp.float32)
    up_pre = jnp.dot(rows_in, w_up, preferred_element_type=jnp.float32)
    act_rows = (jax.nn.silu(gate_pre) * up_pre).astype(jnp.bfloat16)
    out_rows = jnp.dot(act_rows, w_down, preferred_element_type=jnp.float32).astype(jnp.bfloat16)
    return (gate_pre, up_pre, act_rows, out_rows)


def expert_backward(rows_in, gate_pre, up_pre, act_rows, grad_rows, w_gate, w_up, w_down):
    grad_act = jnp.dot(grad_rows, w_down.T, preferred_element_type=jnp.float32)
    sigmoid_gate = jax.nn.sigmoid(gate_pre)
    grad_up_pre = (grad_act * gate_pre * sigmoid_gate).astype(jnp.bfloat16)
    grad_gate_pre = (
        grad_act * up_pre * sigmoid_gate * (1.0 + gate_pre * (1.0 - sigmoid_gate))
    ).astype(jnp.bfloat16)
    grad_down_w = jnp.dot(act_rows.T, grad_rows, preferred_element_type=jnp.float32)
    grad_gate_w = jnp.dot(rows_in.T, grad_gate_pre, preferred_element_type=jnp.float32)
    grad_up_w = jnp.dot(rows_in.T, grad_up_pre, preferred_element_type=jnp.float32)
    grad_rows_in = jnp.dot(grad_gate_pre, w_gate.T, preferred_element_type=jnp.float32)
    grad_rows_in = (
        grad_rows_in + jnp.dot(grad_up_pre, w_up.T, preferred_element_type=jnp.float32)
    ).astype(jnp.bfloat16)
    return (grad_rows_in, grad_gate_w, grad_up_w, grad_down_w)


def axis_bits(size):
    return size.bit_length() - 1


def is_cube(sizes):
    return all(size & (size - 1) == 0 for size in sizes) and sizes[0] > 1


def span(bits):
    masks = [0]
    for bit in bits:
        masks = masks + [mask | (1 << bit) for mask in masks]
    return masks


def stream_orders(sizes):
    dp_bits, fsdp_bits = (axis_bits(sizes[0]), axis_bits(sizes[1]))
    low = [bit for bit in range(fsdp_bits)]
    high = [fsdp_bits + bit for bit in range(dp_bits - 1, 0, -1)]
    core = [fsdp_bits]
    return (high + low + core, high[:-1] + low + high[-1:] + core)


class Cube:
    def __init__(self, sizes):
        self.sizes = sizes
        self.dp = lax.axis_index("dp")
        self.fsdp = lax.axis_index("fsdp")
        self.me = self.dp * sizes[1] + self.fsdp
        self.fsdp_bits = axis_bits(sizes[1])
        self.flips = [
            (1 - 2 * ((self.me // (1 << bit)) % 2)) * (1 << bit)
            for bit in range(axis_bits(sizes[0]) + self.fsdp_bits)
        ]

    def block(self, mask):
        index = self.me
        for bit, flip in enumerate(self.flips):
            if mask >> bit & 1:
                index = index + flip
        return index

    def partner(self, bit):
        other = self.me + self.flips[bit]
        return {"dp": other // self.sizes[1], "fsdp": other % self.sizes[1]}

    def greet(self):
        barrier = pltpu.get_barrier_semaphore()
        for bit in range(len(self.flips)):
            pl.semaphore_signal(
                barrier, inc=1, device_id=self.partner(bit), device_id_type=pl.DeviceIdType.MESH
            )
        pl.semaphore_wait(barrier, len(self.flips))


def gather_kernel(sizes, a_ref, b_ref, a_out, b_out, local_sems, send_sems, recv_sems):
    cube = Cube(sizes)
    cube.greet()
    orders = stream_orders(sizes)
    streams = ((a_ref, a_out), (b_ref, b_out))
    copies = ({}, {})
    arrived = (set(), set())
    own = []
    for which, (source, target) in enumerate(streams):
        own.append(pltpu.make_async_copy(source, target.at[cube.me], local_sems.at[which]))
        own[-1].start()
    for stage in range(len(orders[0])):
        counts = len(span(orders[0][:stage]))
        for place in range(counts):
            for which, (source, target) in enumerate(streams):
                order = orders[which]
                mask = span(order[:stage])[place]
                if mask and mask not in arrived[which]:
                    copies[which][mask].wait_recv()
                    arrived[which].add(mask)
                label = mask | (1 << order[stage])
                copy = pltpu.make_async_remote_copy(
                    src_ref=target.at[cube.block(mask)] if mask else source,
                    dst_ref=target.at[cube.block(mask)],
                    send_sem=send_sems.at[which, label],
                    recv_sem=recv_sems.at[which, label],
                    device_id=cube.partner(order[stage]),
                    device_id_type=pl.DeviceIdType.MESH,
                )
                copy.start()
                copies[which][label] = copy
    for which in range(2):
        for label, copy in copies[which].items():
            if label not in arrived[which]:
                copy.wait_recv()
        for copy in copies[which].values():
            copy.wait_send()
        own[which].wait()


def gather_rows(sizes, packed_a, packed_b):
    blocks = sizes[0] * sizes[1]
    if not is_cube(sizes):
        return tuple(
            lax.all_gather(packed, ("dp", "fsdp"), axis=0) for packed in (packed_a, packed_b)
        )
    return pl.pallas_call(
        lambda *refs: gather_kernel(sizes, *refs),
        out_shape=tuple(
            jax.ShapeDtypeStruct((blocks,) + packed.shape, packed.dtype)
            for packed in (packed_a, packed_b)
        ),
        in_specs=[pl.BlockSpec(memory_space=pl.ANY)] * 2,
        out_specs=(pl.BlockSpec(memory_space=pl.ANY),) * 2,
        scratch_shapes=[
            pltpu.SemaphoreType.DMA((2,)),
            pltpu.SemaphoreType.DMA((2, blocks)),
            pltpu.SemaphoreType.DMA((2, blocks)),
        ],
        compiler_params=pltpu.CompilerParams(collective_id=0, has_side_effects=True),
        name="gather_rows",
    )(packed_a, packed_b)


def scatter_kernel(
    sizes, a_ref, b_ref, a_out, b_out, a_slots, b_slots, a_held, b_held, send_sems, recv_sems
):
    cube = Cube(sizes)
    cube.greet()
    orders = [order[::-1] for order in stream_orders(sizes)]
    streams = ((a_ref, a_out, a_slots, a_held), (b_ref, b_out, b_slots, b_held))
    copies = ({}, {})
    places = ({}, {})

    def total(which, mask, stage):
        source, _, slots, _ = streams[which]
        value = source[cube.block(mask)].astype(jnp.float32)
        for earlier in orders[which][:stage]:
            label = mask | (1 << earlier)
            copies[which][label].wait_recv()
            value = value + slots[label].astype(jnp.float32)
        return value

    for stage in range(len(orders[0])):
        for place in range(len(span(orders[0][stage + 1 :]))):
            for which, (source, _, slots, held) in enumerate(streams):
                order = orders[which]
                masks = span(order[stage + 1 :][::-1])
                masks.sort(
                    key=lambda mask: [
                        at for at, bit in enumerate(order) if mask >> bit & 1
                    ][:1]
                    or [len(order)]
                )
                mask = masks[place] | (1 << order[stage])
                if stage == 0:
                    leaving = source.at[cube.block(mask)]
                else:
                    slot = places[which].setdefault(mask, len(places[which]))
                    held[slot] = total(which, mask, stage).astype(jnp.bfloat16)
                    leaving = held.at[slot]
                copy = pltpu.make_async_remote_copy(
                    src_ref=leaving,
                    dst_ref=slots.at[mask],
                    send_sem=send_sems.at[which, mask],
                    recv_sem=recv_sems.at[which, mask],
                    device_id=cube.partner(order[stage]),
                    device_id_type=pl.DeviceIdType.MESH,
                )
                copy.start()
                copies[which][mask] = copy
    for which, (_, out, _, _) in enumerate(streams):
        out[...] = total(which, 0, len(orders[which]))
    for which in range(2):
        for copy in copies[which].values():
            copy.wait_send()


def scatter_rows(sizes, packed_a, packed_b):
    blocks = sizes[0] * sizes[1]
    if not is_cube(sizes):
        return tuple(
            lax.psum_scatter(packed.astype(jnp.float32), ("dp", "fsdp"), scatter_dimension=0)
            for packed in (packed_a, packed_b)
        )
    shapes = [packed.shape[1:] for packed in (packed_a, packed_b)]
    return pl.pallas_call(
        lambda *refs: scatter_kernel(sizes, *refs),
        out_shape=tuple(jax.ShapeDtypeStruct(shape, jnp.float32) for shape in shapes),
        in_specs=[pl.BlockSpec(memory_space=pltpu.VMEM)] * 2,
        out_specs=(pl.BlockSpec(memory_space=pltpu.VMEM),) * 2,
        scratch_shapes=[
            pltpu.VMEM((blocks,) + shapes[0], jnp.bfloat16),
            pltpu.VMEM((blocks,) + shapes[1], jnp.bfloat16),
            pltpu.VMEM((blocks // 2,) + shapes[0], jnp.bfloat16),
            pltpu.VMEM((blocks // 2,) + shapes[1], jnp.bfloat16),
            pltpu.SemaphoreType.DMA((2, blocks)),
            pltpu.SemaphoreType.DMA((2, blocks)),
        ],
        compiler_params=pltpu.CompilerParams(
            collective_id=1, has_side_effects=True, vmem_limit_bytes=48 * 1024 * 1024
        ),
        name="scatter_rows",
    )(packed_a, packed_b)


def shards(
    sizes,
    hidden_in,
    doc_id,
    expert_ids,
    out_grad,
    attn_gain,
    query_weight,
    key_weight,
    value_weight,
    output_weight,
    ffn_gain,
    router_weight,
    expert_gate,
    expert_up,
    expert_down,
):
    rows = hidden_in.shape[0]
    groups = HEADS // KV_HEADS
    scale = HEAD_DIM ** (-0.5)
    experts_all = router_weight.shape[1]
    query_width, key_width = (query_weight.shape[1], key_weight.shape[1])
    small_width = -(-(experts_all + 2) // 128) * 128
    small = jnp.concatenate([router_weight, attn_gain[:, None], ffn_gain[:, None]], axis=1)
    small = jnp.pad(small, ((0, 0), (0, small_width - small.shape[1])))
    full_a, full_b = gather_rows(
        sizes,
        jnp.concatenate([query_weight, key_weight, small], axis=1),
        jnp.concatenate([value_weight, output_weight], axis=1),
    )
    full_a = full_a.reshape(-1, full_a.shape[2])
    full_b = full_b.reshape(-1, full_b.shape[2])
    w_query = full_a[:, :query_width]
    w_key = full_a[:, query_width : query_width + key_width]
    full_small = full_a[:, query_width + key_width :]
    w_router = full_small[:, :experts_all]
    gain_one, gain_two = (full_small[:, experts_all], full_small[:, experts_all + 1])
    w_value = full_b[:, : value_weight.shape[1]]
    w_output = full_b[:, value_weight.shape[1] :]
    expert_full = (
        lax.all_gather(expert_gate, "fsdp", axis=1, tiled=True),
        lax.all_gather(expert_up, "fsdp", axis=1, tiled=True),
        lax.all_gather(expert_down, "fsdp", axis=1, tiled=True),
    )
    w_gate, w_up, w_down = (expert_full[0][0], expert_full[1][0], expert_full[2][0])
    position, allowed, live_rows = positions_mask(doc_id)
    cosine, sinusoid = rope_tables(position)
    cos_query, sin_query = (cosine[:, None, None, :], sinusoid[:, None, None, :])
    cos_key, sin_key = (cosine[:, None, :], sinusoid[:, None, :])
    resid_in = hidden_in.astype(jnp.float32)
    normed_one, scale_one, normed_in = norm_forward(resid_in, gain_one.astype(jnp.float32))
    query_raw = jnp.dot(normed_in, w_query, preferred_element_type=jnp.float32).reshape(
        rows, KV_HEADS, groups, HEAD_DIM
    )
    key_raw = jnp.dot(normed_in, w_key, preferred_element_type=jnp.float32).reshape(
        rows, KV_HEADS, HEAD_DIM
    )
    query_b = rotate(query_raw, cos_query, sin_query).astype(jnp.bfloat16)
    key_b = rotate(key_raw, cos_key, sin_key).astype(jnp.bfloat16)
    value_b = (
        jnp.dot(normed_in, w_value, preferred_element_type=jnp.float32)
        .reshape(rows, KV_HEADS, HEAD_DIM)
        .astype(jnp.bfloat16)
    )
    probs, log_total = probabilities(query_b, key_b, allowed, None)
    probs_b = probs.astype(jnp.bfloat16)
    mixed = jnp.einsum("kgij,jkd->ikgd", probs_b, value_b, preferred_element_type=jnp.float32)
    mixed_b = (
        (mixed * live_rows[:, None, None, None])
        .reshape(rows, HEADS * HEAD_DIM)
        .astype(jnp.bfloat16)
    )
    resid_mid = resid_in + jnp.dot(mixed_b, w_output, preferred_element_type=jnp.float32)
    normed_two, scale_two, routed_in = norm_forward(resid_mid, gain_two.astype(jnp.float32))
    logits = jnp.dot(routed_in, w_router, preferred_element_type=jnp.float32)
    gates, dispatch, kept, rank = routing(expert_ids, live_rows, logits)
    dispatch_b = dispatch.astype(jnp.bfloat16)
    send_rows = jnp.einsum(
        "ecr,rd->ecd", dispatch_b, routed_in, preferred_element_type=jnp.float32
    ).astype(jnp.bfloat16)
    recv_rows = lax.all_to_all(send_rows, "dp", split_axis=0, concat_axis=0, tiled=True)
    flat_in = recv_rows.reshape(-1, recv_rows.shape[2])
    gate_pre, up_pre, act_rows, out_rows = expert_forward(flat_in, w_gate, w_up, w_down)
    back_rows = lax.all_to_all(
        out_rows.reshape(recv_rows.shape), "dp", split_axis=0, concat_axis=0, tiled=True
    )
    experts = back_rows.shape[0]
    capacity = back_rows.shape[1]
    width = back_rows.shape[2]
    chosen_slot = (expert_ids[:, :, None] == jnp.arange(experts)[None, None, :]).astype(jnp.float32)
    gate_pick = jnp.sum(chosen_slot * (gates * kept)[:, None, :], axis=2)
    rank_pick = jnp.sum(chosen_slot * rank[:, None, :], axis=2)
    slot_index = expert_ids * capacity + jnp.minimum(rank_pick, capacity - 1.0).astype(jnp.int32)
    back_flat = back_rows.reshape(experts * capacity, width)
    picked_rows = jnp.take(back_flat, slot_index.reshape(-1), axis=0).reshape(rows, TOP, width)
    expert_sum = jnp.sum(gate_pick[:, :, None] * picked_rows.astype(jnp.float32), axis=1)
    layer_out = (resid_mid + expert_sum).astype(jnp.bfloat16)
    grad_out = out_grad.astype(jnp.float32)
    slot_gate = jnp.sum(dispatch * gates.T[:, None, :], axis=2)
    pulled_grad = jnp.einsum(
        "ecr,rd->ecd", dispatch_b, out_grad, preferred_element_type=jnp.float32
    )
    grad_send = (slot_gate[:, :, None] * pulled_grad).astype(jnp.bfloat16)
    slot_dot = jnp.sum(back_rows.astype(jnp.float32) * pulled_grad, axis=2)
    grad_gates = jnp.sum(dispatch * slot_dot[:, :, None], axis=1).T
    grad_logits = gates * (grad_gates - jnp.sum(gates * grad_gates, axis=1, keepdims=True))
    grad_logits_b = grad_logits.astype(jnp.bfloat16)
    grad_recv = lax.all_to_all(grad_send, "dp", split_axis=0, concat_axis=0, tiled=True)
    grad_rows_in, grad_gate_w, grad_up_w, grad_down_w = expert_backward(
        flat_in, gate_pre, up_pre, act_rows, grad_recv.reshape(flat_in.shape), w_gate, w_up, w_down
    )
    grad_back = lax.all_to_all(
        grad_rows_in.reshape(recv_rows.shape), "dp", split_axis=0, concat_axis=0, tiled=True
    )
    grad_routed = jnp.einsum(
        "ecr,ecd->rd", dispatch_b, grad_back, preferred_element_type=jnp.float32
    )
    grad_routed = grad_routed + jnp.dot(
        grad_logits_b, w_router.T, preferred_element_type=jnp.float32
    )
    grad_w_router = jnp.dot(routed_in.T, grad_logits_b, preferred_element_type=jnp.float32)
    grad_norm_two, grad_gain_two = norm_backward(
        grad_routed, normed_two, scale_two, gain_two.astype(jnp.float32)
    )
    grad_mid = grad_out + grad_norm_two
    grad_mid_b = grad_mid.astype(jnp.bfloat16)
    grad_w_output = jnp.dot(mixed_b.T, grad_mid_b, preferred_element_type=jnp.float32)
    grad_mixed = jnp.dot(grad_mid_b, w_output.T, preferred_element_type=jnp.float32).reshape(
        rows, KV_HEADS, groups, HEAD_DIM
    )
    grad_mixed = (grad_mixed * live_rows[:, None, None, None]).astype(jnp.bfloat16)
    probs_again, unused_total = probabilities(query_b, key_b, allowed, log_total)
    grad_probs = jnp.einsum(
        "ikgd,jkd->kgij", grad_mixed, value_b, preferred_element_type=jnp.float32
    )
    delta = jnp.sum(probs_again * grad_probs, axis=-1, keepdims=True)
    grad_scores = (probs_again * (grad_probs - delta) * scale).astype(jnp.bfloat16)
    grad_query_raw = jnp.einsum(
        "kgij,jkd->ikgd", grad_scores, key_b, preferred_element_type=jnp.float32
    )
    grad_key_raw = jnp.einsum(
        "kgij,ikgd->jkd", grad_scores, query_b, preferred_element_type=jnp.float32
    )
    grad_value_raw = jnp.einsum(
        "kgij,ikgd->jkd",
        probs_again.astype(jnp.bfloat16),
        grad_mixed,
        preferred_element_type=jnp.float32,
    )
    grad_query_b = (
        unrotate(grad_query_raw, cos_query, sin_query)
        .reshape(rows, HEADS * HEAD_DIM)
        .astype(jnp.bfloat16)
    )
    grad_key_b = (
        unrotate(grad_key_raw, cos_key, sin_key)
        .reshape(rows, KV_HEADS * HEAD_DIM)
        .astype(jnp.bfloat16)
    )
    grad_value_b = grad_value_raw.reshape(rows, KV_HEADS * HEAD_DIM).astype(jnp.bfloat16)
    grad_w_query = jnp.dot(normed_in.T, grad_query_b, preferred_element_type=jnp.float32)
    grad_w_key = jnp.dot(normed_in.T, grad_key_b, preferred_element_type=jnp.float32)
    grad_w_value = jnp.dot(normed_in.T, grad_value_b, preferred_element_type=jnp.float32)
    grad_normed = jnp.dot(grad_query_b, w_query.T, preferred_element_type=jnp.float32)
    grad_normed = grad_normed + jnp.dot(grad_key_b, w_key.T, preferred_element_type=jnp.float32)
    grad_normed = grad_normed + jnp.dot(grad_value_b, w_value.T, preferred_element_type=jnp.float32)
    grad_norm_one, grad_gain_one = norm_backward(
        grad_normed, normed_one, scale_one, gain_one.astype(jnp.float32)
    )
    grad_input = (grad_mid + grad_norm_one).astype(jnp.bfloat16)
    grad_small = jnp.concatenate(
        [grad_w_router, grad_gain_one[:, None], grad_gain_two[:, None]], axis=1
    )
    grad_small = jnp.pad(grad_small, ((0, 0), (0, small_width - grad_small.shape[1])))
    blocks = sizes[0] * sizes[1]
    own_a, own_b = scatter_rows(
        sizes,
        jnp.concatenate(
            [
                grad_w_query.astype(jnp.bfloat16),
                grad_w_key.astype(jnp.bfloat16),
                grad_small.astype(jnp.bfloat16),
            ],
            axis=1,
        ).reshape(blocks, -1, full_a.shape[1]),
        jnp.concatenate(
            [grad_w_value.astype(jnp.bfloat16), grad_w_output.astype(jnp.bfloat16)], axis=1
        ).reshape(blocks, -1, full_b.shape[1]),
    )
    own_small = own_a[:, query_width + key_width :]
    dense_grads = (
        own_small[:, experts_all],
        own_a[:, :query_width],
        own_a[:, query_width : query_width + key_width],
        own_b[:, : value_weight.shape[1]],
        own_b[:, value_weight.shape[1] :],
        own_small[:, experts_all + 1],
        own_small[:, :experts_all],
    )
    expert_grads = (
        lax.psum_scatter(
            grad_gate_w[None].astype(jnp.bfloat16), "fsdp", scatter_dimension=1, tiled=True
        ).astype(jnp.float32),
        lax.psum_scatter(
            grad_up_w[None].astype(jnp.bfloat16), "fsdp", scatter_dimension=1, tiled=True
        ).astype(jnp.float32),
        lax.psum_scatter(
            grad_down_w[None].astype(jnp.bfloat16), "fsdp", scatter_dimension=1, tiled=True
        ).astype(jnp.float32),
    )
    return (
        layer_out,
        grad_input,
        dense_grads[0],
        dense_grads[1],
        dense_grads[2],
        dense_grads[3],
        dense_grads[4],
        dense_grads[5],
        dense_grads[6],
        expert_grads[0],
        expert_grads[1],
        expert_grads[2],
    )


def solution(mesh):
    in_specs = (
        P(("dp", "fsdp"), None),
        P(("dp", "fsdp")),
        P(("dp", "fsdp"), None),
        P(("dp", "fsdp"), None),
        P(("dp", "fsdp")),
        P(("dp", "fsdp"), None),
        P(("dp", "fsdp"), None),
        P(("dp", "fsdp"), None),
        P(("dp", "fsdp"), None),
        P(("dp", "fsdp")),
        P(("dp", "fsdp"), None),
        P("dp", "fsdp", None),
        P("dp", "fsdp", None),
        P("dp", "fsdp", None),
    )
    out_specs = (
        P(("dp", "fsdp"), None),
        P(("dp", "fsdp"), None),
        P(("dp", "fsdp")),
        P(("dp", "fsdp"), None),
        P(("dp", "fsdp"), None),
        P(("dp", "fsdp"), None),
        P(("dp", "fsdp"), None),
        P(("dp", "fsdp")),
        P(("dp", "fsdp"), None),
        P("dp", "fsdp", None),
        P("dp", "fsdp", None),
        P("dp", "fsdp", None),
    )
    sizes = (mesh.shape["dp"], mesh.shape["fsdp"])
    body = functools.partial(shards, sizes)
    return jax.shard_map(body, mesh=mesh, in_specs=in_specs, out_specs=out_specs, check_vma=False)
```

```python
import functools

import jax
import jax.numpy as jnp
from jax import lax
from jax.experimental import pallas as pl
from jax.experimental.pallas import tpu as pltpu
from jax.sharding import PartitionSpec as P

HEADS = 16
KV_HEADS = 8
HEAD_DIM = 64
TOP = 8
CAP = 24


norm_eps = 1e-05


def positions_mask(doc_block):
    row_count = doc_block.shape[0]
    row_index = jnp.arange(row_count)
    same_doc = doc_block[:, None] == doc_block[None, :]
    earlier = row_index[None, :] < row_index[:, None]
    position = jnp.sum((same_doc & earlier).astype(jnp.float32), axis=1)
    allowed = same_doc & (row_index[None, :] <= row_index[:, None])
    live_rows = (doc_block < row_count).astype(jnp.float32)
    return (position, allowed, live_rows)


def rope_tables(position):
    half_dim = HEAD_DIM // 2
    freqs = jnp.exp(-jnp.log(10000.0) * (2.0 * jnp.arange(half_dim, dtype=jnp.float32) / HEAD_DIM))
    angle = position[:, None] * freqs[None, :]
    return (jnp.cos(angle), jnp.sin(angle))


def rotate(values, cosine, sinusoid):
    half_dim = values.shape[-1] // 2
    first_half, second_half = (values[..., :half_dim], values[..., half_dim:])
    return jnp.concatenate(
        [
            first_half * cosine - second_half * sinusoid,
            second_half * cosine + first_half * sinusoid,
        ],
        axis=-1,
    )


def unrotate(values, cosine, sinusoid):
    half_dim = values.shape[-1] // 2
    first_half, second_half = (values[..., :half_dim], values[..., half_dim:])
    return jnp.concatenate(
        [
            first_half * cosine + second_half * sinusoid,
            second_half * cosine - first_half * sinusoid,
        ],
        axis=-1,
    )


def norm_forward(values, gain):
    scale_row = lax.rsqrt(jnp.mean(values * values, axis=-1, keepdims=True) + norm_eps)
    normed = values * scale_row
    return (normed, scale_row, (normed * gain).astype(jnp.bfloat16))


def norm_backward(upstream, normed, scale_row, gain):
    scaled = upstream * gain
    inner = jnp.mean(scaled * normed, axis=-1, keepdims=True)
    return (scale_row * (scaled - normed * inner), jnp.sum(upstream * normed, axis=0))


def probabilities(query_b, key_b, allowed, log_total):
    scores = jnp.einsum(
        "ikgd,jkd->kgij", query_b, key_b, preferred_element_type=jnp.float32
    ) * HEAD_DIM ** (-0.5)
    raised = jnp.where(allowed[None, None], jnp.exp(scores), 0.0)
    if log_total is None:
        log_total = jnp.log(jnp.sum(raised, axis=-1, keepdims=True))
    return (jnp.where(allowed[None, None], jnp.exp(scores - log_total), 0.0), log_total)


def routing(expert_block, live_rows, logits):
    experts = logits.shape[1]
    row_count = expert_block.shape[0]
    chosen = jnp.sum(
        (expert_block[:, :, None] == jnp.arange(experts)[None, None, :]).astype(jnp.float32), axis=1
    )
    raised = jnp.where(chosen > 0, jnp.exp(logits), 0.0)
    gates = raised / jnp.sum(raised, axis=1, keepdims=True)
    member = chosen * live_rows[:, None]
    lower = (jnp.arange(row_count)[None, :] < jnp.arange(row_count)[:, None]).astype(jnp.float32)
    rank = jnp.dot(lower, member, precision=lax.Precision.HIGHEST)
    kept = member * (rank < CAP).astype(jnp.float32)
    slot_match = (rank.T[:, None, :] == jnp.arange(CAP, dtype=jnp.float32)[None, :, None]).astype(
        jnp.float32
    )
    dispatch = kept.T[:, None, :] * slot_match
    return (gates, dispatch, kept, rank)


def expert_forward(rows_in, w_gate, w_up, w_down):
    gate_pre = jnp.dot(rows_in, w_gate, preferred_element_type=jnp.float32)
    up_pre = jnp.dot(rows_in, w_up, preferred_element_type=jnp.float32)
    act_rows = (jax.nn.silu(gate_pre) * up_pre).astype(jnp.bfloat16)
    out_rows = jnp.dot(act_rows, w_down, preferred_element_type=jnp.float32).astype(jnp.bfloat16)
    return (gate_pre, up_pre, act_rows, out_rows)


def expert_backward(rows_in, gate_pre, up_pre, act_rows, grad_rows, w_gate, w_up, w_down):
    grad_act = jnp.dot(grad_rows, w_down.T, preferred_element_type=jnp.float32)
    sigmoid_gate = jax.nn.sigmoid(gate_pre)
    grad_up_pre = (grad_act * gate_pre * sigmoid_gate).astype(jnp.bfloat16)
    grad_gate_pre = (
        grad_act * up_pre * sigmoid_gate * (1.0 + gate_pre * (1.0 - sigmoid_gate))
    ).astype(jnp.bfloat16)
    grad_down_w = jnp.dot(act_rows.T, grad_rows, preferred_element_type=jnp.float32)
    grad_gate_w = jnp.dot(rows_in.T, grad_gate_pre, preferred_element_type=jnp.float32)
    grad_up_w = jnp.dot(rows_in.T, grad_up_pre, preferred_element_type=jnp.float32)
    grad_rows_in = jnp.dot(grad_gate_pre, w_gate.T, preferred_element_type=jnp.float32)
    grad_rows_in = (
        grad_rows_in + jnp.dot(grad_up_pre, w_up.T, preferred_element_type=jnp.float32)
    ).astype(jnp.bfloat16)
    return (grad_rows_in, grad_gate_w, grad_up_w, grad_down_w)


def axis_bits(size):
    return size.bit_length() - 1


def is_cube(sizes):
    return all(size & (size - 1) == 0 for size in sizes) and sizes[0] > 1


def span(bits):
    masks = [0]
    for bit in bits:
        masks = masks + [mask | (1 << bit) for mask in masks]
    return masks


def stream_orders(sizes):
    dp_bits, fsdp_bits = (axis_bits(sizes[0]), axis_bits(sizes[1]))
    low = [bit for bit in range(fsdp_bits)]
    high = [fsdp_bits + bit for bit in range(dp_bits - 1, 0, -1)]
    core = [fsdp_bits]
    return (
        high[:-1] + low + high[-1:] + core,
        high[:-2] + low + high[-1:] + high[-2:-1] + core,
    )


class Cube:
    def __init__(self, sizes):
        self.sizes = sizes
        self.dp = lax.axis_index("dp")
        self.fsdp = lax.axis_index("fsdp")
        self.me = self.dp * sizes[1] + self.fsdp
        self.fsdp_bits = axis_bits(sizes[1])
        self.flips = [
            (1 - 2 * ((self.me // (1 << bit)) % 2)) * (1 << bit)
            for bit in range(axis_bits(sizes[0]) + self.fsdp_bits)
        ]

    def block(self, mask):
        index = self.me
        for bit, flip in enumerate(self.flips):
            if mask >> bit & 1:
                index = index + flip
        return index

    def partner(self, bit):
        other = self.me + self.flips[bit]
        return {"dp": other // self.sizes[1], "fsdp": other % self.sizes[1]}

    def greet(self):
        barrier = pltpu.get_barrier_semaphore()
        for bit in range(len(self.flips)):
            pl.semaphore_signal(
                barrier, inc=1, device_id=self.partner(bit), device_id_type=pl.DeviceIdType.MESH
            )
        pl.semaphore_wait(barrier, len(self.flips))


def gather_kernel(sizes, a_ref, b_ref, a_out, b_out, local_sems, send_sems, recv_sems):
    cube = Cube(sizes)
    cube.greet()
    orders = stream_orders(sizes)
    streams = ((a_ref, a_out), (b_ref, b_out))
    copies = ({}, {})
    arrived = (set(), set())
    own = []
    for which, (source, target) in enumerate(streams):
        own.append(pltpu.make_async_copy(source, target.at[cube.me], local_sems.at[which]))
        own[-1].start()
    stages = len(orders[0])
    places = sorted(range(1 << stages), key=lambda place: (place.bit_count(), place))
    for place in places:
        for which, (source, target) in enumerate(streams):
            order = orders[which]
            mask = span(order)[place]
            later = range(place.bit_length(), stages)
            if mask and len(later):
                copies[which][mask].wait_recv()
                arrived[which].add(mask)
            for stage in later:
                label = mask | (1 << order[stage])
                copy = pltpu.make_async_remote_copy(
                    src_ref=target.at[cube.block(mask)] if mask else source,
                    dst_ref=target.at[cube.block(mask)],
                    send_sem=send_sems.at[which, label],
                    recv_sem=recv_sems.at[which, label],
                    device_id=cube.partner(order[stage]),
                    device_id_type=pl.DeviceIdType.MESH,
                )
                copy.start()
                copies[which][label] = copy
    for which in range(2):
        for label, copy in copies[which].items():
            if label not in arrived[which]:
                copy.wait_recv()
        for copy in copies[which].values():
            copy.wait_send()
        own[which].wait()


def gather_rows(sizes, packed_a, packed_b):
    blocks = sizes[0] * sizes[1]
    if not is_cube(sizes):
        return tuple(
            lax.all_gather(packed, ("dp", "fsdp"), axis=0) for packed in (packed_a, packed_b)
        )
    return pl.pallas_call(
        lambda *refs: gather_kernel(sizes, *refs),
        out_shape=tuple(
            jax.ShapeDtypeStruct((blocks,) + packed.shape, packed.dtype)
            for packed in (packed_a, packed_b)
        ),
        in_specs=[pl.BlockSpec(memory_space=pl.ANY)] * 2,
        out_specs=(pl.BlockSpec(memory_space=pl.ANY),) * 2,
        scratch_shapes=[
            pltpu.SemaphoreType.DMA((2,)),
            pltpu.SemaphoreType.DMA((2, blocks)),
            pltpu.SemaphoreType.DMA((2, blocks)),
        ],
        compiler_params=pltpu.CompilerParams(collective_id=0, has_side_effects=True),
        name="gather_rows",
    )(packed_a, packed_b)


def scatter_kernel(sizes, width, *refs):
    cube = Cube(sizes)
    cube.greet()
    two_orders = [order[::-1] for order in stream_orders(sizes)]
    orders = [two_orders[which % 2] for which in range(width)]
    streams = [refs[which : 4 * width : width] for which in range(width)]
    send_sems, recv_sems = refs[4 * width :]
    copies = [{} for _ in range(width)]
    places = [{} for _ in range(width)]

    def total(which, mask, stage):
        source, _, slots, _ = streams[which]
        value = source[cube.block(mask)].astype(jnp.float32)
        for earlier in orders[which][:stage]:
            label = mask | (1 << earlier)
            copies[which][label].wait_recv()
            value = value + slots[label].astype(jnp.float32)
        return value

    for stage in range(len(orders[0])):
        for place in range(len(span(orders[0][stage + 1 :]))):
            for which, (source, _, slots, held) in enumerate(streams):
                order = orders[which]
                masks = span(order[stage + 1 :][::-1])
                masks.sort(
                    key=lambda mask: [
                        at for at, bit in enumerate(order) if mask >> bit & 1
                    ][:1]
                    or [len(order)]
                )
                mask = masks[place] | (1 << order[stage])
                if stage == 0:
                    leaving = source.at[cube.block(mask)]
                else:
                    slot = places[which].setdefault(mask, len(places[which]))
                    held[slot] = total(which, mask, stage).astype(jnp.bfloat16)
                    leaving = held.at[slot]
                copy = pltpu.make_async_remote_copy(
                    src_ref=leaving,
                    dst_ref=slots.at[mask],
                    send_sem=send_sems.at[which, mask],
                    recv_sem=recv_sems.at[which, mask],
                    device_id=cube.partner(order[stage]),
                    device_id_type=pl.DeviceIdType.MESH,
                )
                copy.start()
                copies[which][mask] = copy
    for which, (_, out, _, _) in enumerate(streams):
        out[...] = total(which, 0, len(orders[which]))
    for which in range(width):
        for copy in copies[which].values():
            copy.wait_send()


def scatter_rows(sizes, *grads):
    blocks = sizes[0] * sizes[1]
    packed = [grad.reshape((blocks, -1) + grad.shape[1:]) for grad in grads]
    if not is_cube(sizes):
        return tuple(
            lax.psum_scatter(part.astype(jnp.float32), ("dp", "fsdp"), scatter_dimension=0)
            for part in packed
        )
    width = len(packed)
    shapes = [part.shape[1:] for part in packed]
    return pl.pallas_call(
        lambda *refs: scatter_kernel(sizes, width, *refs),
        out_shape=tuple(jax.ShapeDtypeStruct(shape, jnp.float32) for shape in shapes),
        in_specs=[pl.BlockSpec(memory_space=pltpu.VMEM)] * width,
        out_specs=(pl.BlockSpec(memory_space=pltpu.VMEM),) * width,
        scratch_shapes=[pltpu.VMEM((blocks,) + shape, jnp.bfloat16) for shape in shapes]
        + [pltpu.VMEM((blocks // 2,) + shape, jnp.bfloat16) for shape in shapes]
        + [pltpu.SemaphoreType.DMA((width, blocks))] * 2,
        compiler_params=pltpu.CompilerParams(
            collective_id=1, has_side_effects=True, vmem_limit_bytes=48 * 1024 * 1024
        ),
        name="scatter_rows",
    )(*packed)


def shards(
    sizes,
    hidden_in,
    doc_id,
    expert_ids,
    out_grad,
    attn_gain,
    query_weight,
    key_weight,
    value_weight,
    output_weight,
    ffn_gain,
    router_weight,
    expert_gate,
    expert_up,
    expert_down,
):
    rows = hidden_in.shape[0]
    groups = HEADS // KV_HEADS
    scale = HEAD_DIM ** (-0.5)
    experts_all = router_weight.shape[1]
    query_width, key_width = (query_weight.shape[1], key_weight.shape[1])
    small_width = -(-(experts_all + 2) // 128) * 128
    small = jnp.concatenate([router_weight, attn_gain[:, None], ffn_gain[:, None]], axis=1)
    small = jnp.pad(small, ((0, 0), (0, small_width - small.shape[1])))
    full_a, full_b = gather_rows(
        sizes,
        jnp.concatenate([query_weight, key_weight, small], axis=1),
        jnp.concatenate([value_weight, output_weight], axis=1),
    )
    full_a = full_a.reshape(-1, full_a.shape[2])
    full_b = full_b.reshape(-1, full_b.shape[2])
    w_query = full_a[:, :query_width]
    w_key = full_a[:, query_width : query_width + key_width]
    full_small = full_a[:, query_width + key_width :]
    w_router = full_small[:, :experts_all]
    gain_one, gain_two = (full_small[:, experts_all], full_small[:, experts_all + 1])
    w_value = full_b[:, : value_weight.shape[1]]
    w_output = full_b[:, value_weight.shape[1] :]
    expert_full = (
        lax.all_gather(expert_gate, "fsdp", axis=1, tiled=True),
        lax.all_gather(expert_up, "fsdp", axis=1, tiled=True),
        lax.all_gather(expert_down, "fsdp", axis=1, tiled=True),
    )
    w_gate, w_up, w_down = (expert_full[0][0], expert_full[1][0], expert_full[2][0])
    position, allowed, live_rows = positions_mask(doc_id)
    cosine, sinusoid = rope_tables(position)
    cos_query, sin_query = (cosine[:, None, None, :], sinusoid[:, None, None, :])
    cos_key, sin_key = (cosine[:, None, :], sinusoid[:, None, :])
    resid_in = hidden_in.astype(jnp.float32)
    normed_one, scale_one, normed_in = norm_forward(resid_in, gain_one.astype(jnp.float32))
    query_raw = jnp.dot(normed_in, w_query, preferred_element_type=jnp.float32).reshape(
        rows, KV_HEADS, groups, HEAD_DIM
    )
    key_raw = jnp.dot(normed_in, w_key, preferred_element_type=jnp.float32).reshape(
        rows, KV_HEADS, HEAD_DIM
    )
    query_b = rotate(query_raw, cos_query, sin_query).astype(jnp.bfloat16)
    key_b = rotate(key_raw, cos_key, sin_key).astype(jnp.bfloat16)
    value_b = (
        jnp.dot(normed_in, w_value, preferred_element_type=jnp.float32)
        .reshape(rows, KV_HEADS, HEAD_DIM)
        .astype(jnp.bfloat16)
    )
    probs, log_total = probabilities(query_b, key_b, allowed, None)
    probs_b = probs.astype(jnp.bfloat16)
    mixed = jnp.einsum("kgij,jkd->ikgd", probs_b, value_b, preferred_element_type=jnp.float32)
    mixed_b = (
        (mixed * live_rows[:, None, None, None])
        .reshape(rows, HEADS * HEAD_DIM)
        .astype(jnp.bfloat16)
    )
    resid_mid = resid_in + jnp.dot(mixed_b, w_output, preferred_element_type=jnp.float32)
    normed_two, scale_two, routed_in = norm_forward(resid_mid, gain_two.astype(jnp.float32))
    logits = jnp.dot(routed_in, w_router, preferred_element_type=jnp.float32)
    gates, dispatch, kept, rank = routing(expert_ids, live_rows, logits)
    dispatch_b = dispatch.astype(jnp.bfloat16)
    send_rows = jnp.einsum(
        "ecr,rd->ecd", dispatch_b, routed_in, preferred_element_type=jnp.float32
    ).astype(jnp.bfloat16)
    slot_gate = jnp.sum(dispatch * gates.T[:, None, :], axis=2)
    pulled_grad = jnp.einsum(
        "ecr,rd->ecd", dispatch_b, out_grad, preferred_element_type=jnp.float32
    )
    grad_send = (slot_gate[:, :, None] * pulled_grad).astype(jnp.bfloat16)
    recv_both = lax.all_to_all(
        jnp.concatenate([send_rows, grad_send], axis=1),
        "dp",
        split_axis=0,
        concat_axis=0,
        tiled=True,
    )
    recv_rows, grad_recv = jnp.split(recv_both, 2, axis=1)
    flat_in = recv_rows.reshape(-1, recv_rows.shape[2])
    gate_pre, up_pre, act_rows, out_rows = expert_forward(flat_in, w_gate, w_up, w_down)
    back_rows = lax.all_to_all(
        out_rows.reshape(recv_rows.shape), "dp", split_axis=0, concat_axis=0, tiled=True
    )
    experts = back_rows.shape[0]
    capacity = back_rows.shape[1]
    width = back_rows.shape[2]
    chosen_slot = (expert_ids[:, :, None] == jnp.arange(experts)[None, None, :]).astype(jnp.float32)
    gate_pick = jnp.sum(chosen_slot * (gates * kept)[:, None, :], axis=2)
    rank_pick = jnp.sum(chosen_slot * rank[:, None, :], axis=2)
    slot_index = expert_ids * capacity + jnp.minimum(rank_pick, capacity - 1.0).astype(jnp.int32)
    back_flat = back_rows.reshape(experts * capacity, width)
    picked_rows = jnp.take(back_flat, slot_index.reshape(-1), axis=0).reshape(rows, TOP, width)
    expert_sum = jnp.sum(gate_pick[:, :, None] * picked_rows.astype(jnp.float32), axis=1)
    layer_out = (resid_mid + expert_sum).astype(jnp.bfloat16)
    grad_out = out_grad.astype(jnp.float32)
    slot_dot = jnp.sum(back_rows.astype(jnp.float32) * pulled_grad, axis=2)
    grad_gates = jnp.sum(dispatch * slot_dot[:, :, None], axis=1).T
    grad_logits = gates * (grad_gates - jnp.sum(gates * grad_gates, axis=1, keepdims=True))
    grad_logits_b = grad_logits.astype(jnp.bfloat16)
    grad_rows_in, grad_gate_w, grad_up_w, grad_down_w = expert_backward(
        flat_in, gate_pre, up_pre, act_rows, grad_recv.reshape(flat_in.shape), w_gate, w_up, w_down
    )
    grad_back = lax.all_to_all(
        grad_rows_in.reshape(recv_rows.shape), "dp", split_axis=0, concat_axis=0, tiled=True
    )
    grad_routed = jnp.einsum(
        "ecr,ecd->rd", dispatch_b, grad_back, preferred_element_type=jnp.float32
    )
    grad_routed = grad_routed + jnp.dot(
        grad_logits_b, w_router.T, preferred_element_type=jnp.float32
    )
    grad_w_router = jnp.dot(routed_in.T, grad_logits_b, preferred_element_type=jnp.float32)
    grad_norm_two, grad_gain_two = norm_backward(
        grad_routed, normed_two, scale_two, gain_two.astype(jnp.float32)
    )
    grad_mid = grad_out + grad_norm_two
    grad_mid_b = grad_mid.astype(jnp.bfloat16)
    grad_w_output = jnp.dot(mixed_b.T, grad_mid_b, preferred_element_type=jnp.float32)
    grad_mixed = jnp.dot(grad_mid_b, w_output.T, preferred_element_type=jnp.float32).reshape(
        rows, KV_HEADS, groups, HEAD_DIM
    )
    grad_mixed = (grad_mixed * live_rows[:, None, None, None]).astype(jnp.bfloat16)
    probs_again, unused_total = probabilities(query_b, key_b, allowed, log_total)
    grad_probs = jnp.einsum(
        "ikgd,jkd->kgij", grad_mixed, value_b, preferred_element_type=jnp.float32
    )
    delta = jnp.sum(probs_again * grad_probs, axis=-1, keepdims=True)
    grad_scores = (probs_again * (grad_probs - delta) * scale).astype(jnp.bfloat16)
    grad_query_raw = jnp.einsum(
        "kgij,jkd->ikgd", grad_scores, key_b, preferred_element_type=jnp.float32
    )
    grad_key_raw = jnp.einsum(
        "kgij,ikgd->jkd", grad_scores, query_b, preferred_element_type=jnp.float32
    )
    grad_value_raw = jnp.einsum(
        "kgij,ikgd->jkd",
        probs_again.astype(jnp.bfloat16),
        grad_mixed,
        preferred_element_type=jnp.float32,
    )
    grad_query_b = (
        unrotate(grad_query_raw, cos_query, sin_query)
        .reshape(rows, HEADS * HEAD_DIM)
        .astype(jnp.bfloat16)
    )
    grad_key_b = (
        unrotate(grad_key_raw, cos_key, sin_key)
        .reshape(rows, KV_HEADS * HEAD_DIM)
        .astype(jnp.bfloat16)
    )
    grad_value_b = grad_value_raw.reshape(rows, KV_HEADS * HEAD_DIM).astype(jnp.bfloat16)
    grad_w_query_key = jnp.dot(
        normed_in.T,
        jnp.concatenate([grad_query_b, grad_key_b], axis=1),
        preferred_element_type=jnp.float32,
    )
    grad_w_value = jnp.dot(normed_in.T, grad_value_b, preferred_element_type=jnp.float32)
    grad_normed = jnp.dot(grad_query_b, w_query.T, preferred_element_type=jnp.float32)
    grad_normed = grad_normed + jnp.dot(grad_key_b, w_key.T, preferred_element_type=jnp.float32)
    grad_normed = grad_normed + jnp.dot(grad_value_b, w_value.T, preferred_element_type=jnp.float32)
    grad_norm_one, grad_gain_one = norm_backward(
        grad_normed, normed_one, scale_one, gain_one.astype(jnp.float32)
    )
    grad_input = (grad_mid + grad_norm_one).astype(jnp.bfloat16)
    grad_small = jnp.concatenate(
        [grad_w_router, grad_gain_one[:, None], grad_gain_two[:, None]], axis=1
    )
    grad_small = jnp.pad(grad_small, ((0, 0), (0, small_width - grad_small.shape[1])))
    own_qk, own_output, own_small, own_value = scatter_rows(
        sizes,
        grad_w_query_key.astype(jnp.bfloat16),
        grad_w_output.astype(jnp.bfloat16),
        grad_small.astype(jnp.bfloat16),
        grad_w_value.astype(jnp.bfloat16),
    )
    dense_grads = (
        own_small[:, experts_all],
        own_qk[:, :query_width],
        own_qk[:, query_width:],
        own_value,
        own_output,
        own_small[:, experts_all + 1],
        own_small[:, :experts_all],
    )
    expert_grads = (
        lax.psum_scatter(
            grad_gate_w[None].astype(jnp.bfloat16), "fsdp", scatter_dimension=1, tiled=True
        ).astype(jnp.float32),
        lax.psum_scatter(
            grad_up_w[None].astype(jnp.bfloat16), "fsdp", scatter_dimension=1, tiled=True
        ).astype(jnp.float32),
        lax.psum_scatter(
            grad_down_w[None].astype(jnp.bfloat16), "fsdp", scatter_dimension=1, tiled=True
        ).astype(jnp.float32),
    )
    return (
        layer_out,
        grad_input,
        dense_grads[0],
        dense_grads[1],
        dense_grads[2],
        dense_grads[3],
        dense_grads[4],
        dense_grads[5],
        dense_grads[6],
        expert_grads[0],
        expert_grads[1],
        expert_grads[2],
    )


def solution(mesh):
    in_specs = (
        P(("dp", "fsdp"), None),
        P(("dp", "fsdp")),
        P(("dp", "fsdp"), None),
        P(("dp", "fsdp"), None),
        P(("dp", "fsdp")),
        P(("dp", "fsdp"), None),
        P(("dp", "fsdp"), None),
        P(("dp", "fsdp"), None),
        P(("dp", "fsdp"), None),
        P(("dp", "fsdp")),
        P(("dp", "fsdp"), None),
        P("dp", "fsdp", None),
        P("dp", "fsdp", None),
        P("dp", "fsdp", None),
    )
    out_specs = (
        P(("dp", "fsdp"), None),
        P(("dp", "fsdp"), None),
        P(("dp", "fsdp")),
        P(("dp", "fsdp"), None),
        P(("dp", "fsdp"), None),
        P(("dp", "fsdp"), None),
        P(("dp", "fsdp"), None),
        P(("dp", "fsdp")),
        P(("dp", "fsdp"), None),
        P("dp", "fsdp", None),
        P("dp", "fsdp", None),
        P("dp", "fsdp", None),
    )
    sizes = (mesh.shape["dp"], mesh.shape["fsdp"])
    body = functools.partial(shards, sizes)
    return jax.shard_map(body, mesh=mesh, in_specs=in_specs, out_specs=out_specs, check_vma=False)
```
